32 devices in a mesh: frow: 4 (over z), fcol: 4 (over x, core), chan: 2 (over y).
Axes of the slice: x: 2, y: 2, z: 4, core: 2. Of those that a mesh axis runs over, the one named last changes fastest.
Arguments:
- image_cube: float32 [32, 256, 1024], P('chan', 'frow', 'fcol'), may hold values from -40 to 40
- weights: float32 [3, 256, 1024], P(None, 'frow', 'fcol'), may hold values from 0.5 to 2
Outputs:
- backprojected: float32 [32, 256, 1024], P('chan', 'frow', 'fcol')
- lowrank: float32 [32, 256, 1024], P('chan', 'frow', 'fcol')
The draws below stay inside these ranges and needn't reach their ends.
All inputs are finite; a program needn't handle non-finite values.
Results may differ from the reference program's by a relative error of at most 0.0003.
Values sent between devices are 32-bit elements; how exact they have to be, the bound alone decides.
A program may use at most 128 MiB of HBM per device.

```python
import math
import jax
import jax.numpy as jnp
import numpy as np
from jax import lax

L = 32
CR = 64
CC = 256
JSWEEPS = 3
NR = 256
NC = 1024
N_FROW = 4
N_FCOL = 4


def draw_image_cube(key, part):
    subkeys = jax.random.split(key, 4)
    noise_part = jax.random.normal(subkeys[0], (L, NR, NC), jnp.float32)
    spectra = 0.7 * jax.random.normal(subkeys[1], (L, 4), jnp.float32)
    sky_maps = jax.random.normal(subkeys[2], (4, NR, NC), jnp.float32)
    rough_part = jax.random.uniform(subkeys[3], (L,), jnp.float32, 0.7, 1.3)
    channel_ramp = 3.0 ** (jnp.arange(L, dtype=jnp.float32) / (L - 1))
    amplitude = channel_ramp * rough_part
    mixture = noise_part + jnp.einsum('lk,kij->lij', spectra, sky_maps)
    return jnp.clip(amplitude[:, None, None] * mixture, -40.0, 40.0).astype(jnp.float32)


def steps_of(stream_key, shape, pieces, smallest, high):
    level, own = 1.0, jax.random.fold_in(stream_key, 6)
    for axis_at, parts in pieces:
        steps = jnp.exp(jax.random.uniform(jax.random.fold_in(own, axis_at), (parts,), jnp.float32, smallest / len(pieces), high / len(pieces)))
        level = level * jnp.repeat(steps, shape[axis_at] // parts).reshape([-1 if axis == axis_at else 1 for axis in range(len(shape))])
    return level


def setup_inputs(seed: int = 0) -> dict:
    arg_keys = jax.random.split(jax.random.key(seed), 3)
    image_cube = draw_image_cube(jax.random.fold_in(arg_keys[2], 71), 0)
    weights = jnp.clip(jnp.exp(math.log(2.0) - 1.3862944 * jax.random.uniform(arg_keys[1], (3, NR, NC), jnp.float32) ** steps_of(arg_keys[1], (3, NR, NC), ((1, 4), (2, 4)), -0.2, 0.2)), 0.5, 2.0)
    return dict(image_cube=image_cube, weights=weights)


filter_taps = (0.0625, 0.25, 0.375, 0.25, 0.0625)
band_levels = (12.0, 4.0, 2.5)
rank_level = 2.0
tiny_value = 1e-30

def smooth(extended, dilation):
    reach_cells = 2 * dilation
    row_count = extended.shape[-2] - 2 * reach_cells
    col_count = extended.shape[-1] - 2 * reach_cells
    across = filter_taps[0] * extended[..., 0:row_count, :]
    for tap_index in range(1, 5):
        offset = tap_index * dilation
        across = across + filter_taps[tap_index] * extended[..., offset:offset + row_count, :]
    result = filter_taps[0] * across[..., 0:col_count]
    for tap_index in range(1, 5):
        offset = tap_index * dilation
        result = result + filter_taps[tap_index] * across[..., offset:offset + col_count]
    return result

def tournament(order_size):
    players = list(range(order_size))
    tables = []
    for round_index in range(order_size - 1):
        first_list = []
        second_list = []
        for slot_index in range(order_size // 2):
            left_one = players[slot_index]
            right_one = players[order_size - 1 - slot_index]
            first_list.append(min(left_one, right_one))
            second_list.append(max(left_one, right_one))
        order_list = np.array(first_list + second_list, np.int32)
        inverse_list = np.argsort(order_list).astype(np.int32)
        tables.append((np.array(first_list, np.int32), np.array(second_list, np.int32), order_list, inverse_list))
        players = [players[0], players[-1]] + players[1:-1]
    return tables

def jacobi(gram_matrix):
    order_size = gram_matrix.shape[0]
    half_size = order_size // 2
    tables = tournament(order_size)
    identity_matrix = jnp.eye(order_size, dtype=gram_matrix.dtype)

    def one_round(matrix, vectors, first_list, second_list, order_list, inverse_list):
        diag_values = jnp.diagonal(matrix)
        left_diag = diag_values[first_list]
        right_diag = diag_values[second_list]
        cross_term = matrix[first_list, second_list]
        gap_value = right_diag - left_diag
        sign_part = jnp.where(gap_value >= 0, 1.0, -1.0)
        tangent = sign_part * 2.0 * cross_term / (jnp.abs(gap_value) + jnp.sqrt(gap_value * gap_value + 4.0 * cross_term * cross_term) + tiny_value)
        cosine = 1.0 / jnp.sqrt(1.0 + tangent * tangent)
        sine_part = tangent * cosine

        def turn_columns(block):
            placed = block[:, order_list]
            left_cols = placed[:, :half_size]
            right_cols = placed[:, half_size:]
            turned = jnp.concatenate([cosine * left_cols - sine_part * right_cols, sine_part * left_cols + cosine * right_cols], axis=1)
            return turned[:, inverse_list]
        matrix = turn_columns(matrix)
        matrix = turn_columns(matrix.T).T
        vectors = turn_columns(vectors)
        return (matrix, vectors)

    def sweep(counter, carried):
        matrix, vectors = carried
        for first_list, second_list, order_list, inverse_list in tables:
            matrix, vectors = one_round(matrix, vectors, first_list, second_list, order_list, inverse_list)
        return (matrix, vectors)
    matrix, vectors = lax.fori_loop(0, JSWEEPS, sweep, (gram_matrix, identity_matrix))
    return (jnp.diagonal(matrix), vectors)

def spectral_map(gram_matrix, threshold):
    values, vectors = jacobi(gram_matrix)
    factors = 1.0 - threshold / jnp.sqrt(jnp.maximum(values, threshold * threshold))
    return jnp.dot(vectors * factors[None, :], vectors.T, precision=lax.Precision.HIGHEST)

def reference(image_cube, weights):
    channels = image_cube.shape[0]
    coarse_one = smooth(jnp.pad(image_cube, ((0, 0), (2, 2), (2, 2))), 1)
    coarse_two = smooth(jnp.pad(coarse_one, ((0, 0), (4, 4), (4, 4))), 2)
    band_list = (image_cube - coarse_one, coarse_one - coarse_two, coarse_two)
    dual_list = []
    for band_index in range(3):
        levels = band_levels[band_index] * weights[band_index]
        totals = lax.optimization_barrier(jnp.sum(band_list[band_index] * band_list[band_index], axis=0))
        dual_list.append(band_list[band_index] * (levels / jnp.sqrt(jnp.maximum(totals, levels * levels))))
    inner_part = smooth(jnp.pad(dual_list[2] - dual_list[1], ((0, 0), (4, 4), (4, 4))), 2)
    summed = dual_list[1] - dual_list[0] + inner_part
    backprojected = dual_list[0] + smooth(jnp.pad(summed, ((0, 0), (2, 2), (2, 2))), 1)
    pixels = CR * CC
    threshold = rank_level * math.sqrt(pixels)
    facets = image_cube.reshape(channels, N_FROW, CR, N_FCOL, CC).transpose(1, 3, 0, 2, 4).reshape(N_FROW * N_FCOL, channels, pixels)

    def project(matrix):
        gram_matrix = jnp.dot(matrix, matrix.T, precision=lax.Precision.HIGHEST)
        mixing = spectral_map(gram_matrix, threshold)
        return jnp.dot(mixing, matrix, precision=lax.Precision.HIGHEST)
    projected = lax.map(project, facets)
    lowrank = projected.reshape(N_FROW, N_FCOL, channels, CR, CC).transpose(2, 0, 3, 1, 4).reshape(channels, N_FROW * CR, N_FCOL * CC)
    return (backprojected, lowrank)
```

```python
import functools
import math

import jax
import jax.numpy as jnp
from jax import lax
from jax.experimental import pallas as pl
from jax.experimental.pallas import tpu as pltpu
from jax.sharding import PartitionSpec as P

JSWEEPS = 3


filter_taps = (0.0625, 0.25, 0.375, 0.25, 0.0625)
band_levels = (12.0, 4.0, 2.5)
rank_level = 2.0
tiny_value = 1e-30


def rank_round(state, marks):
    quads, sides, labels, cosine, sine = state
    eye, lane, row, first_mask, last_mask, step_mask, last = marks
    upper_left, upper_right, lower_left, lower_right = quads
    side_top, side_bottom = sides
    label_top, label_bottom = labels

    def across(values):
        return jnp.sum(jnp.where(eye, values, 0.0), axis=0, keepdims=True)

    cosine_row = across(cosine)
    sine_row = across(sine)

    def turn_rows(top, bottom):
        return cosine * top - sine * bottom, sine * top + cosine * bottom

    def move_rows(top, bottom):
        up = pltpu.roll(jnp.where(row == 0, bottom, top), 1, 0)
        down = pltpu.roll(bottom, last, 0)
        return jnp.where(row == 0, top, up), jnp.where(row == last, top, down)

    def turn_cols(left, right):
        return cosine_row * left - sine_row * right, sine_row * left + cosine_row * right

    def move_cols(left, right):
        ahead = pltpu.roll(jnp.where(lane == 0, right, left), 1, 1)
        back = pltpu.roll(right, lane.shape[1] - 1, 1)
        return jnp.where(lane == 0, left, ahead), jnp.where(lane == last, left, back)

    upper_left, lower_left = move_rows(*turn_rows(upper_left, lower_left))
    upper_right, lower_right = move_rows(*turn_rows(upper_right, lower_right))
    upper_left, upper_right = turn_cols(upper_left, upper_right)
    lower_left, lower_right = turn_cols(lower_left, lower_right)
    sides = move_rows(*turn_rows(side_top, side_bottom))
    label_top, label_bottom = move_rows(label_top, label_bottom)
    own_top = jnp.where(step_mask, upper_left, jnp.where(first_mask, upper_right, 0.0))
    next_mask = lane == row + 1
    own_bottom = jnp.where(
        next_mask & (row < last), lower_right, jnp.where(last_mask, lower_left, 0.0)
    )
    pair = jnp.where(next_mask & (row < last), upper_right, jnp.where(last_mask, upper_left, 0.0))
    gap = jnp.sum(own_bottom - own_top, axis=1, keepdims=True)
    cross = jnp.sum(pair, axis=1, keepdims=True)
    cosine, sine = turn_of(gap, cross, label_top < label_bottom)
    upper = move_cols(upper_left, upper_right)
    lower = move_cols(lower_left, lower_right)
    return (upper + lower, sides, (label_top, label_bottom), cosine, sine)


def turn_of(gap, cross, ordered):
    gap = jnp.broadcast_to(gap, ordered.shape)
    cross = jnp.broadcast_to(cross, ordered.shape)
    positive = (gap > 0) | ((gap == 0) & ordered)
    double = 2.0 * cross
    root = jnp.sqrt(gap * gap + double * double)
    tangent = jnp.where(positive, double, -double) / (jnp.abs(gap) + root + tiny_value)
    cosine = lax.rsqrt(1.0 + tangent * tangent)
    return cosine, tangent * cosine


def rank_start(gram):
    order = gram.shape[0]
    half, last, lanes = order // 2, order // 2 - 1, 128
    highest = lax.Precision.HIGHEST
    row = lax.broadcasted_iota(jnp.int32, (half, lanes), 0)
    lane = lax.broadcasted_iota(jnp.int32, (half, lanes), 1)
    eye = lane == row
    first_mask = (row == 1) & (lane == 0)
    last_mask = (row == last) & (lane == last)
    step_mask = ((row == 0) & (lane == 0)) | ((row >= 2) & (lane == row - 1))
    marks = (eye, lane, row, first_mask, last_mask, step_mask, last)
    mirror = lane == order - 1 - row
    pick_row = lax.broadcasted_iota(jnp.int32, (order, lanes), 0)
    pick_lane = lax.broadcasted_iota(jnp.int32, (order, lanes), 1)
    one = lambda mask: jnp.where(mask, 1.0, 0.0)
    pick_left = one((pick_row == pick_lane) & (pick_lane < half))
    pick_right = one((pick_row == order - 1 - pick_lane) & (pick_lane < half))
    dot = functools.partial(jnp.dot, precision=highest, preferred_element_type=jnp.float32)
    flip_row = lax.broadcasted_iota(jnp.int32, (half, half), 0)
    flip_lane = lax.broadcasted_iota(jnp.int32, (half, half), 1)
    flip = one(flip_row + flip_lane == last)
    top, bottom = gram[:half], dot(flip, gram[half:])
    quads = (dot(top, pick_left), dot(top, pick_right), dot(bottom, pick_left), dot(bottom, pick_right))
    sides = (one(eye), one(mirror))
    labels = (row, order - 1 - row)
    total = lambda values: jnp.sum(jnp.where(eye, values, 0.0), axis=1, keepdims=True)
    cosine, sine = turn_of(
        total(quads[3] - quads[0]), total(quads[1]), labels[0] < labels[1]
    )
    return (quads, sides, labels, cosine, sine), marks


def rank_finish(state, marks, threshold):
    highest = lax.Precision.HIGHEST
    eye = marks[0]
    total = lambda values: jnp.sum(jnp.where(eye, values, 0.0), axis=1, keepdims=True)
    quads, sides = state[0], state[1]
    mixing = 0.0
    for quad, side in zip((quads[0], quads[3]), sides):
        values = total(quad)
        factor = 1.0 - threshold / jnp.sqrt(jnp.maximum(values, threshold * threshold))
        mixing = mixing + lax.dot_general(
            side * factor, side, (((0,), (0,)), ((), ())), precision=highest,
            preferred_element_type=jnp.float32,
        )
    order = 2 * eye.shape[0]
    return mixing[:order, :order]


def spread(x, dilation):
    for axis in (0, 1):
        size = x.shape[axis]
        total = filter_taps[2] * x
        for step in (1, 2):
            shift = step * dilation
            near = pltpu.roll(x, shift, axis) + pltpu.roll(x, size - shift, axis)
            total = total + filter_taps[2 - step] * near
        x = total
    return x


def split_two(values):
    high = values.astype(jnp.bfloat16)
    low = (values - high.astype(jnp.float32)).astype(jnp.bfloat16)
    return high, low


def facet_kernel(
    threshold, image_ref, flat_ref, weights_ref, back_ref, rank_ref,
    wide, bands, sums, other_sums, diffs, full, gram, other_gram, mixing,
    pack_out, pack_in, pack_out_two, pack_in_two, send_sems, recv_sems, local_sems,
):
    channels, rows, cols = image_ref.shape
    pixels = rows * cols
    part = pixels // 2
    names = ("frow", "fcol", "chan")
    place = {name: lax.axis_index(name) for name in names}
    count = {name: lax.axis_size(name) for name in names}
    me = place["chan"]
    partner = 1 - me
    has = {
        ("frow", 1): place["frow"] < count["frow"] - 1,
        ("frow", -1): place["frow"] > 0,
        ("fcol", 1): place["fcol"] < count["fcol"] - 1,
        ("fcol", -1): place["fcol"] > 0,
    }
    barrier = pltpu.get_barrier_semaphore()
    mesh_ids = pl.DeviceIdType.MESH

    def target(name, step):
        ids = dict(place)
        ids[name] = place[name] + step
        return tuple(ids[key] for key in names)

    def mate():
        return (place["frow"], place["fcol"], partner)

    def copy_to(index, source, sink, device):
        return pltpu.make_async_remote_copy(
            src_ref=source, dst_ref=sink, send_sem=send_sems.at[index],
            recv_sem=recv_sems.at[index], device_id=device, device_id_type=mesh_ids,
        )

    own_rows = pl.ds(pl.multiple_of(me * channels, channels), channels)
    to_mate = pl.ds(pl.multiple_of(partner * part, part), part)
    to_self = pl.ds(pl.multiple_of(me * part, part), part)
    keep_flat = pltpu.make_async_copy(flat_ref, full.at[own_rows, :], local_sems.at[0])
    keep_image = pltpu.make_async_copy(
        image_ref, wide.at[:, pl.ds(8, rows), :], local_sems.at[1]
    )
    keep_flat.start()
    keep_image.start()

    zero_rows = jnp.zeros((channels, 8, cols), jnp.float32)

    @pl.when(jnp.logical_not(has["frow", -1]))
    def _():
        wide[:, 0:8, :] = zero_rows
        diffs[0, :, 0:8, :] = zero_rows
        diffs[1, :, 0:8, :] = zero_rows

    @pl.when(jnp.logical_not(has["frow", 1]))
    def _():
        wide[:, rows + 8 : rows + 16, :] = zero_rows
        diffs[0, :, rows + 8 : rows + 16, :] = zero_rows
        diffs[1, :, rows + 8 : rows + 16, :] = zero_rows

    for side, step in ((0, -1), (1, 1)):

        @pl.when(jnp.logical_not(has["fcol", step]))
        def _(side=side):
            pack_in[side] = jnp.zeros(pack_in.shape[1:], jnp.float32)
            pack_in_two[side] = jnp.zeros(pack_in_two.shape[1:], jnp.float32)

    pl.semaphore_signal(barrier, inc=1, device_id=mate(), device_id_type=mesh_ids)
    friends = 1
    for key in has:

        @pl.when(has[key])
        def _(key=key):
            pl.semaphore_signal(barrier, inc=1, device_id=target(*key), device_id_type=mesh_ids)

        friends = friends + jnp.where(has[key], 1, 0)
    pl.semaphore_wait(barrier, friends)

    first_part = copy_to(0, flat_ref.at[:, to_mate], full.at[own_rows, to_mate], mate())
    second_part = copy_to(1, flat_ref.at[:, to_self], full.at[own_rows, to_self], mate())
    below = lambda ref, at: ref.at[..., pl.ds(at, 8), :]

    def row_copies(index, source, offset, sink):
        return (
            (("frow", 1), ("frow", -1), copy_to(
                index, below(source, offset + rows - 8), below(sink, 0), target("frow", 1))),
            (("frow", -1), ("frow", 1), copy_to(
                index + 1, below(source, offset), below(sink, rows + 8), target("frow", -1))),
        )

    def col_copies(index, source, sink):
        return (
            (("fcol", 1), ("fcol", -1), copy_to(
                index, source.at[1], sink.at[0], target("fcol", 1))),
            (("fcol", -1), ("fcol", 1), copy_to(
                index + 1, source.at[0], sink.at[1], target("fcol", -1))),
        )

    def start_all(copies):
        for goes, _, copy in copies:

            @pl.when(has[goes])
            def _(copy=copy):
                copy.start()

    def arrive_all(copies):
        for _, comes, copy in copies:

            @pl.when(has[comes])
            def _(copy=copy):
                copy.wait_recv()

    def left_all(copies):
        for goes, _, copy in copies:

            @pl.when(has[goes])
            def _(copy=copy):
                copy.wait_send()

    rows_one = row_copies(2, image_ref, 0, wide)
    cols_one = col_copies(4, pack_out, pack_in)
    rows_two = row_copies(8, diffs, 8, diffs)
    cols_two = col_copies(10, pack_out_two, pack_in_two)
    start_all(rows_one)
    first_part.start()

    tall = rows + 16
    tile_lane = lax.broadcasted_iota(jnp.int32, (tall, 128), 1)

    def pack_edges(load, store):
        def body(ch, sides):
            left, right = sides
            here = (tile_lane >= ch * 8) & (tile_lane < ch * 8 + 8)
            tile_first = pltpu.roll(load(ch, pl.ds(0, 128)), ch * 8, 1)
            tile_last = pltpu.roll(load(ch, pl.ds(cols - 128, 128)), ch * 8 + 8, 1)
            return jnp.where(here, tile_first, left), jnp.where(here, tile_last, right)

        empty = jnp.zeros((tall, 128), jnp.float32)
        left, right = lax.fori_loop(0, channels, body, (empty, empty))
        store(0, left)
        store(1, right)

    def edge_tile(ch, before, after):
        after = pltpu.roll(after, 128 - ch * 8, 1)
        before = pltpu.roll(before, 120 - ch * 8, 1)
        return jnp.where(tile_lane < 8, after, jnp.where(tile_lane >= 120, before, 0.0))

    long = cols + 128
    row_at = lax.broadcasted_iota(jnp.int32, (tall, long), 0) - 8
    col_at = lax.broadcasted_iota(jnp.int32, (tall, long), 1)
    col_at = jnp.where(col_at < cols + 64, col_at, col_at - long)
    row_at = row_at + place["frow"] * rows
    col_at = col_at + place["fcol"] * cols
    valid = (row_at >= 0) & (row_at < count["frow"] * rows)
    valid = valid & (col_at >= 0) & (col_at < count["fcol"] * cols)
    inside = lambda values: jnp.where(valid, values, 0.0)

    keep_image.wait()
    arrive_all(rows_one)
    pack_edges(lambda ch, at: wide[ch, :, at], pack_out.__setitem__)
    start_all(cols_one)
    sums[...] = jnp.zeros(sums.shape, jnp.float32)
    arrive_all(cols_one)

    def analyse(ch, carried):
        center = wide[ch]
        tile = edge_tile(ch, pack_in[0], pack_in[1])
        coarse_one = inside(spread(jnp.concatenate([center, tile], axis=1), 1))
        coarse_two = spread(coarse_one, 2)[8 : rows + 8, :cols]
        coarse_one = coarse_one[8 : rows + 8, :cols]
        for index, band in enumerate(
            (center[8 : rows + 8] - coarse_one, coarse_one - coarse_two, coarse_two)
        ):
            bands[index, ch] = band
            sums[index] = sums[index] + band * band
        return carried

    lax.fori_loop(0, channels, analyse, 0)
    share_sums = copy_to(6, sums, other_sums, mate())

    keep_flat.wait()
    first_part.wait_recv()
    order = 2 * channels
    block = 1024
    start = me * part

    def gram_step(step, total):
        at = pl.ds(pl.multiple_of(start + step * block, block), block)
        both = jnp.concatenate(split_two(full[:, at]), axis=0)
        return total + lax.dot_general(
            both, both, (((1,), (1,)), ((), ())), preferred_element_type=jnp.float32
        )

    product = lax.fori_loop(
        0, part // block, gram_step, jnp.zeros((2 * order, 2 * order), jnp.float32)
    )
    gram[:, :order] = (
        product[:order, :order] + (product[:order, order:] + product[order:, :order])
    ) + product[order:, order:]
    share_gram = copy_to(7, gram, other_gram, mate())
    share_gram.start()

    share_sums.start()
    second_part.start()

    share_gram.wait_recv()
    state, marks = rank_start(gram[:, :order] + other_gram[:, :order])
    rounds = JSWEEPS * (order - 1)
    turn = lambda _, carried: rank_round(carried, marks)
    state = lax.fori_loop(0, 3 * rounds // 10, turn, state)
    share_sums.wait_recv()
    for index in range(3):
        levels = band_levels[index] * weights_ref[index]
        totals = sums[index] + other_sums[index]
        other_sums[index] = levels / jnp.sqrt(jnp.maximum(totals, levels * levels))

    def project(ch, carried):
        duals = [bands[index, ch] * other_sums[index] for index in range(3)]
        back_ref[ch] = duals[0]
        diffs[0, ch, pl.ds(8, rows), :] = duals[1] - duals[0]
        diffs[1, ch, pl.ds(8, rows), :] = duals[2] - duals[1]
        return carried

    lax.fori_loop(0, channels, project, 0)
    start_all(rows_two)
    state = lax.fori_loop(3 * rounds // 10, 8 * rounds // 10, turn, state)
    arrive_all(rows_two)
    for index in range(2):
        pack_edges(
            lambda ch, at, index=index: diffs[index, ch, :, at],
            lambda side, value, index=index: pack_out_two.__setitem__((side, index), value),
        )
    start_all(cols_two)
    state = lax.fori_loop(8 * rounds // 10, rounds, turn, state)
    mixing[:, :order] = rank_finish(state, marks, threshold)

    arrive_all(cols_two)

    def synthesise(ch, carried):
        outer, inner = [
            jnp.concatenate(
                [diffs[index, ch], edge_tile(ch, pack_in_two[0, index], pack_in_two[1, index])],
                axis=1,
            )
            for index in range(2)
        ]
        summed = inside(outer + spread(inner, 2))
        back_ref[ch] = back_ref[ch] + spread(summed, 1)[8 : rows + 8, :cols]
        return carried

    lax.fori_loop(0, channels, synthesise, 0)

    second_part.wait_recv()
    high, low = split_two(mixing[own_rows, :order])
    left = jnp.concatenate([high, high, low, low], axis=1)

    def rank_step(step, carried):
        at = pl.ds(pl.multiple_of(step * block, block), block)
        high, low = split_two(full[:, at])
        right = jnp.concatenate([high, low, high, low], axis=0)
        rank_ref[:, at] = jnp.dot(left, right, preferred_element_type=jnp.float32)
        return carried

    lax.fori_loop(0, pixels // block, rank_step, 0)
    for copies in (rows_one, cols_one, rows_two, cols_two):
        left_all(copies)
    for copy in (first_part, second_part, share_sums, share_gram):
        copy.wait_send()


def shards(image_cube, weights):
    channels, rows, cols = image_cube.shape
    pixels = rows * cols
    threshold = rank_level * math.sqrt(pixels)
    order = channels * lax.axis_size("chan")
    tall = rows + 16
    f32 = jnp.float32
    anywhere = pl.BlockSpec(memory_space=pl.ANY)
    in_vmem = pl.BlockSpec(memory_space=pltpu.VMEM)
    back, rank = pl.pallas_call(
        functools.partial(facet_kernel, threshold),
        out_shape=(
            jax.ShapeDtypeStruct(image_cube.shape, f32),
            jax.ShapeDtypeStruct((channels, pixels), f32),
        ),
        in_specs=[anywhere, anywhere, in_vmem],
        out_specs=(in_vmem, in_vmem),
        scratch_shapes=[
            pltpu.VMEM((channels, tall, cols), f32),
            pltpu.VMEM((3, channels, rows, cols), f32),
            pltpu.VMEM((3, rows, cols), f32),
            pltpu.VMEM((3, rows, cols), f32),
            pltpu.VMEM((2, channels, tall, cols), f32),
            pltpu.VMEM((order, pixels), f32),
            pltpu.VMEM((order, 128), f32),
            pltpu.VMEM((order, 128), f32),
            pltpu.VMEM((order, 128), f32),
            pltpu.VMEM((2, tall, 128), f32),
            pltpu.VMEM((2, tall, 128), f32),
            pltpu.VMEM((2, 2, tall, 128), f32),
            pltpu.VMEM((2, 2, tall, 128), f32),
            pltpu.SemaphoreType.DMA((12,)),
            pltpu.SemaphoreType.DMA((12,)),
            pltpu.SemaphoreType.DMA((2,)),
        ],
        compiler_params=pltpu.CompilerParams(
            collective_id=0, has_side_effects=True, vmem_limit_bytes=50 * 2**20
        ),
    )(image_cube, image_cube.reshape(channels, pixels), weights)
    return back, rank.reshape(image_cube.shape)


def solution(mesh):
    placed = (P("chan", "frow", "fcol"), P(None, "frow", "fcol"))
    return jax.shard_map(
        shards,
        mesh=mesh,
        in_specs=placed,
        out_specs=(P("chan", "frow", "fcol"), P("chan", "frow", "fcol")),
        check_vma=False,
    )
```

```python
import functools
import math

import jax
import jax.numpy as jnp
from jax import lax
from jax.experimental import pallas as pl
from jax.experimental.pallas import tpu as pltpu
from jax.sharding import PartitionSpec as P

JSWEEPS = 3


filter_taps = (0.0625, 0.25, 0.375, 0.25, 0.0625)
band_levels = (12.0, 4.0, 2.5)
rank_level = 2.0
tiny_value = 1e-30


def rank_round(state, marks):
    quads, sides, labels, cosine, sine = state
    eye, lane, row, first_mask, last_mask, step_mask, last = marks
    upper_left, upper_right, lower_left, lower_right = quads
    side_top, side_bottom = sides
    label_top, label_bottom = labels

    def across(values):
        return jnp.sum(jnp.where(eye, values, 0.0), axis=0, keepdims=True)

    cosine_row = across(cosine)
    sine_row = across(sine)

    def turn_rows(top, bottom):
        return cosine * top - sine * bottom, sine * top + cosine * bottom

    def move_rows(top, bottom):
        up = pltpu.roll(jnp.where(row == 0, bottom, top), 1, 0)
        down = pltpu.roll(bottom, last, 0)
        return jnp.where(row == 0, top, up), jnp.where(row == last, top, down)

    def turn_cols(left, right):
        return cosine_row * left - sine_row * right, sine_row * left + cosine_row * right

    def move_cols(left, right):
        ahead = pltpu.roll(jnp.where(lane == 0, right, left), 1, 1)
        back = pltpu.roll(right, lane.shape[1] - 1, 1)
        return jnp.where(lane == 0, left, ahead), jnp.where(lane == last, left, back)

    upper_left, lower_left = move_rows(*turn_rows(upper_left, lower_left))
    upper_right, lower_right = move_rows(*turn_rows(upper_right, lower_right))
    upper_left, upper_right = turn_cols(upper_left, upper_right)
    lower_left, lower_right = turn_cols(lower_left, lower_right)
    sides = move_rows(*turn_rows(side_top, side_bottom))
    label_top, label_bottom = move_rows(label_top, label_bottom)
    own_top = jnp.where(step_mask, upper_left, jnp.where(first_mask, upper_right, 0.0))
    next_mask = lane == row + 1
    own_bottom = jnp.where(
        next_mask & (row < last), lower_right, jnp.where(last_mask, lower_left, 0.0)
    )
    pair = jnp.where(next_mask & (row < last), upper_right, jnp.where(last_mask, upper_left, 0.0))
    gap = jnp.sum(own_bottom - own_top, axis=1, keepdims=True)
    cross = jnp.sum(pair, axis=1, keepdims=True)
    cosine, sine = turn_of(gap, cross, label_top < label_bottom)
    upper = move_cols(upper_left, upper_right)
    lower = move_cols(lower_left, lower_right)
    return (upper + lower, sides, (label_top, label_bottom), cosine, sine)


def turn_of(gap, cross, ordered):
    gap = jnp.broadcast_to(gap, ordered.shape)
    cross = jnp.broadcast_to(cross, ordered.shape)
    positive = (gap > 0) | ((gap == 0) & ordered)
    double = 2.0 * cross
    root = jnp.sqrt(gap * gap + double * double)
    tangent = jnp.where(positive, double, -double) / (jnp.abs(gap) + root + tiny_value)
    cosine = lax.rsqrt(1.0 + tangent * tangent)
    return cosine, tangent * cosine


def rank_start(gram):
    order = gram.shape[0]
    half, last, lanes = order // 2, order // 2 - 1, 128
    highest = lax.Precision.HIGHEST
    row = lax.broadcasted_iota(jnp.int32, (half, lanes), 0)
    lane = lax.broadcasted_iota(jnp.int32, (half, lanes), 1)
    eye = lane == row
    first_mask = (row == 1) & (lane == 0)
    last_mask = (row == last) & (lane == last)
    step_mask = ((row == 0) & (lane == 0)) | ((row >= 2) & (lane == row - 1))
    marks = (eye, lane, row, first_mask, last_mask, step_mask, last)
    mirror = lane == order - 1 - row
    pick_row = lax.broadcasted_iota(jnp.int32, (order, lanes), 0)
    pick_lane = lax.broadcasted_iota(jnp.int32, (order, lanes), 1)
    one = lambda mask: jnp.where(mask, 1.0, 0.0)
    pick_left = one((pick_row == pick_lane) & (pick_lane < half))
    pick_right = one((pick_row == order - 1 - pick_lane) & (pick_lane < half))
    dot = functools.partial(jnp.dot, precision=highest, preferred_element_type=jnp.float32)
    flip_row = lax.broadcasted_iota(jnp.int32, (half, half), 0)
    flip_lane = lax.broadcasted_iota(jnp.int32, (half, half), 1)
    flip = one(flip_row + flip_lane == last)
    top, bottom = gram[:half], dot(flip, gram[half:])
    quads = (dot(top, pick_left), dot(top, pick_right), dot(bottom, pick_left), dot(bottom, pick_right))
    sides = (one(eye), one(mirror))
    labels = (row, order - 1 - row)
    total = lambda values: jnp.sum(jnp.where(eye, values, 0.0), axis=1, keepdims=True)
    cosine, sine = turn_of(
        total(quads[3] - quads[0]), total(quads[1]), labels[0] < labels[1]
    )
    return (quads, sides, labels, cosine, sine), marks


def rank_finish(state, marks, threshold):
    highest = lax.Precision.HIGHEST
    eye = marks[0]
    total = lambda values: jnp.sum(jnp.where(eye, values, 0.0), axis=1, keepdims=True)
    quads, sides = state[0], state[1]
    mixing = 0.0
    for quad, side in zip((quads[0], quads[3]), sides):
        values = total(quad)
        factor = 1.0 - threshold / jnp.sqrt(jnp.maximum(values, threshold * threshold))
        mixing = mixing + lax.dot_general(
            side * factor, side, (((0,), (0,)), ((), ())), precision=highest,
            preferred_element_type=jnp.float32,
        )
    order = 2 * eye.shape[0]
    return mixing[:order, :order]


def spread(x, dilation):
    for axis in (0, 1):
        size = x.shape[axis]
        pair = x + pltpu.roll(x, 2 * dilation, axis)
        ends = pair + pltpu.roll(pair, size - 2 * dilation, axis)
        x = ends + 4.0 * (x + pltpu.roll(pair, size - dilation, axis))
    return x * (filter_taps[0] * filter_taps[0])


def split_two(values):
    high = values.astype(jnp.bfloat16)
    low = (values - high.astype(jnp.float32)).astype(jnp.bfloat16)
    return high, low


def facet_kernel(
    threshold, image_ref, weights_ref, back_ref, rank_ref,
    wide, bands, sums, other_sums, diffs, full, gram, other_gram, mixing,
    pack_out, pack_in, pack_out_two, pack_in_two, send_sems, recv_sems, local_sems,
):
    channels, rows, cols = image_ref.shape
    pixels = rows * cols
    part = pixels // 2
    names = ("frow", "fcol", "chan")
    place = {name: lax.axis_index(name) for name in names}
    count = {name: lax.axis_size(name) for name in names}
    me = place["chan"]
    partner = 1 - me
    has = {
        ("frow", 1): place["frow"] < count["frow"] - 1,
        ("frow", -1): place["frow"] > 0,
        ("fcol", 1): place["fcol"] < count["fcol"] - 1,
        ("fcol", -1): place["fcol"] > 0,
    }
    barrier = pltpu.get_barrier_semaphore()
    mesh_ids = pl.DeviceIdType.MESH

    def target(name, step):
        ids = dict(place)
        ids[name] = place[name] + step
        return tuple(ids[key] for key in names)

    def mate():
        return (place["frow"], place["fcol"], partner)

    def copy_to(index, source, sink, device):
        return pltpu.make_async_remote_copy(
            src_ref=source, dst_ref=sink, send_sem=send_sems.at[index],
            recv_sem=recv_sems.at[index], device_id=device, device_id_type=mesh_ids,
        )

    own_rows = pl.ds(pl.multiple_of(me * channels, channels), channels)
    to_mate = pl.ds(pl.multiple_of(partner * part, part), part)
    to_self = pl.ds(pl.multiple_of(me * part, part), part)
    keep_image = pltpu.make_async_copy(
        image_ref, wide.at[:, pl.ds(8, rows), :], local_sems.at[0]
    )
    keep_image.start()

    zero_rows = jnp.zeros((channels, 8, cols), jnp.float32)

    @pl.when(jnp.logical_not(has["frow", -1]))
    def _():
        wide[:, 0:8, :] = zero_rows
        diffs[0, :, 0:8, :] = zero_rows
        diffs[1, :, 0:8, :] = zero_rows

    @pl.when(jnp.logical_not(has["frow", 1]))
    def _():
        wide[:, rows + 8 : rows + 16, :] = zero_rows
        diffs[0, :, rows + 8 : rows + 16, :] = zero_rows
        diffs[1, :, rows + 8 : rows + 16, :] = zero_rows

    for side, step in ((0, -1), (1, 1)):

        @pl.when(jnp.logical_not(has["fcol", step]))
        def _(side=side):
            pack_in[side] = jnp.zeros(pack_in.shape[1:], jnp.float32)
            pack_in_two[side] = jnp.zeros(pack_in_two.shape[1:], jnp.float32)

    pl.semaphore_signal(barrier, inc=1, device_id=mate(), device_id_type=mesh_ids)
    friends = 1
    for key in has:

        @pl.when(has[key])
        def _(key=key):
            pl.semaphore_signal(barrier, inc=1, device_id=target(*key), device_id_type=mesh_ids)

        friends = friends + jnp.where(has[key], 1, 0)
    pl.semaphore_wait(barrier, friends)

    first_part = copy_to(0, full.at[own_rows, to_mate], full.at[own_rows, to_mate], mate())
    second_part = copy_to(1, full.at[own_rows, to_self], full.at[own_rows, to_self], mate())
    below = lambda ref, at: ref.at[..., pl.ds(at, 8), :]

    def row_copies(index, source, offset, sink):
        return (
            (("frow", 1), ("frow", -1), copy_to(
                index, below(source, offset + rows - 8), below(sink, 0), target("frow", 1))),
            (("frow", -1), ("frow", 1), copy_to(
                index + 1, below(source, offset), below(sink, rows + 8), target("frow", -1))),
        )

    def col_copies(index, source, sink):
        return (
            (("fcol", 1), ("fcol", -1), copy_to(
                index, source.at[1], sink.at[0], target("fcol", 1))),
            (("fcol", -1), ("fcol", 1), copy_to(
                index + 1, source.at[0], sink.at[1], target("fcol", -1))),
        )

    def start_all(copies):
        for goes, _, copy in copies:

            @pl.when(has[goes])
            def _(copy=copy):
                copy.start()

    def arrive_all(copies):
        for _, comes, copy in copies:

            @pl.when(has[comes])
            def _(copy=copy):
                copy.wait_recv()

    def left_all(copies):
        for goes, _, copy in copies:

            @pl.when(has[goes])
            def _(copy=copy):
                copy.wait_send()

    rows_one = row_copies(2, image_ref, 0, wide)
    cols_one = col_copies(4, pack_out, pack_in)
    rows_two = row_copies(8, diffs, 8, diffs)
    cols_two = col_copies(10, pack_out_two, pack_in_two)
    start_all(rows_one)
    keep_image.wait()

    def flatten(at):
        group = jnp.swapaxes(wide[:, pl.ds(pl.multiple_of(at + 8, 8), 8), :], 0, 1)
        for row in range(8):
            where = pl.multiple_of((at + row) * cols, cols)
            full[own_rows, pl.ds(where, cols)] = group[row]

    def flatten_part(which):
        def body(step, carried):
            flatten(pl.multiple_of(which * (rows // 2) + step * 8, 8))
            return carried

        lax.fori_loop(0, rows // 16, body, 0)

    flatten_part(partner)
    first_part.start()
    flatten_part(me)

    tall = rows + 16
    tile_lane = lax.broadcasted_iota(jnp.int32, (tall, 128), 1)

    def pack_edges(load, store):
        def body(ch, sides):
            left, right = sides
            here = (tile_lane >= ch * 8) & (tile_lane < ch * 8 + 8)
            tile_first = pltpu.roll(load(ch, pl.ds(0, 128)), ch * 8, 1)
            tile_last = pltpu.roll(load(ch, pl.ds(cols - 128, 128)), ch * 8 + 8, 1)
            return jnp.where(here, tile_first, left), jnp.where(here, tile_last, right)

        empty = jnp.zeros((tall, 128), jnp.float32)
        left, right = lax.fori_loop(0, channels, body, (empty, empty))
        store(0, left)
        store(1, right)

    def edge_tile(ch, before, after):
        after = pltpu.roll(after, 128 - ch * 8, 1)
        before = pltpu.roll(before, 120 - ch * 8, 1)
        return jnp.where(tile_lane < 8, after, jnp.where(tile_lane >= 120, before, 0.0))

    long = cols + 128
    row_at = lax.broadcasted_iota(jnp.int32, (tall, long), 0) - 8
    col_at = lax.broadcasted_iota(jnp.int32, (tall, long), 1)
    col_at = jnp.where(col_at < cols + 64, col_at, col_at - long)
    row_at = row_at + place["frow"] * rows
    col_at = col_at + place["fcol"] * cols
    valid = (row_at >= 0) & (row_at < count["frow"] * rows)
    valid = valid & (col_at >= 0) & (col_at < count["fcol"] * cols)
    inside = lambda values: jnp.where(valid, values, 0.0)

    arrive_all(rows_one)
    pack_edges(lambda ch, at: wide[ch, :, at], pack_out.__setitem__)
    start_all(cols_one)
    sums[...] = jnp.zeros(sums.shape, jnp.float32)
    arrive_all(cols_one)

    def analyse(ch, carried):
        center = wide[ch]
        tile = edge_tile(ch, pack_in[0], pack_in[1])
        coarse_one = inside(spread(jnp.concatenate([center, tile], axis=1), 1))
        coarse_two = spread(coarse_one, 2)[8 : rows + 8, :cols]
        coarse_one = coarse_one[8 : rows + 8, :cols]
        for index, band in enumerate(
            (center[8 : rows + 8] - coarse_one, coarse_one - coarse_two, coarse_two)
        ):
            bands[index, ch] = band
            sums[index] = sums[index] + band * band
        return carried

    lax.fori_loop(0, channels, analyse, 0)
    share_sums = copy_to(6, sums, other_sums, mate())

    first_part.wait_recv()
    order = 2 * channels
    block = 1024
    start = me * part

    def gram_step(step, total):
        at = pl.ds(pl.multiple_of(start + step * block, block), block)
        both = jnp.concatenate(split_two(full[:, at]), axis=0)
        return total + lax.dot_general(
            both, both, (((1,), (1,)), ((), ())), preferred_element_type=jnp.float32
        )

    product = lax.fori_loop(
        0, part // block, gram_step, jnp.zeros((2 * order, 2 * order), jnp.float32)
    )
    gram[:, :order] = (
        product[:order, :order] + (product[:order, order:] + product[order:, :order])
    ) + product[order:, order:]
    share_gram = copy_to(7, gram, other_gram, mate())
    share_gram.start()

    share_sums.start()
    second_part.start()

    share_gram.wait_recv()
    state, marks = rank_start(gram[:, :order] + other_gram[:, :order])
    rounds = JSWEEPS * (order - 1)
    turn = lambda _, carried: rank_round(carried, marks)
    state = lax.fori_loop(0, 3 * rounds // 10, turn, state)
    share_sums.wait_recv()
    for index in range(3):
        levels = band_levels[index] * weights_ref[index]
        totals = sums[index] + other_sums[index]
        other_sums[index] = levels / jnp.sqrt(jnp.maximum(totals, levels * levels))

    def project(ch, carried):
        duals = [bands[index, ch] * other_sums[index] for index in range(3)]
        back_ref[ch] = duals[0]
        diffs[0, ch, pl.ds(8, rows), :] = duals[1] - duals[0]
        diffs[1, ch, pl.ds(8, rows), :] = duals[2] - duals[1]
        return carried

    lax.fori_loop(0, channels, project, 0)
    start_all(rows_two)
    state = lax.fori_loop(3 * rounds // 10, 8 * rounds // 10, turn, state)
    arrive_all(rows_two)
    for index in range(2):
        pack_edges(
            lambda ch, at, index=index: diffs[index, ch, :, at],
            lambda side, value, index=index: pack_out_two.__setitem__((side, index), value),
        )
    start_all(cols_two)
    state = lax.fori_loop(8 * rounds // 10, rounds, turn, state)
    mixing[:, :order] = rank_finish(state, marks, threshold)

    arrive_all(cols_two)

    def synthesise(ch, carried):
        outer, inner = [
            jnp.concatenate(
                [diffs[index, ch], edge_tile(ch, pack_in_two[0, index], pack_in_two[1, index])],
                axis=1,
            )
            for index in range(2)
        ]
        summed = inside(outer + spread(inner, 2))
        back_ref[ch] = back_ref[ch] + spread(summed, 1)[8 : rows + 8, :cols]
        return carried

    lax.fori_loop(0, channels, synthesise, 0)

    second_part.wait_recv()
    high, low = split_two(mixing[own_rows, :order])
    left = jnp.concatenate([high, high, low, low], axis=1)

    def rank_step(step, carried):
        at = pl.ds(pl.multiple_of(step * block, block), block)
        high, low = split_two(full[:, at])
        right = jnp.concatenate([high, low, high, low], axis=0)
        rank_ref[:, at] = jnp.dot(left, right, preferred_element_type=jnp.float32)
        return carried

    lax.fori_loop(0, pixels // block, rank_step, 0)
    for copies in (rows_one, cols_one, rows_two, cols_two):
        left_all(copies)
    for copy in (first_part, second_part, share_sums, share_gram):
        copy.wait_send()


def shards(image_cube, weights):
    channels, rows, cols = image_cube.shape
    pixels = rows * cols
    threshold = rank_level * math.sqrt(pixels)
    order = channels * lax.axis_size("chan")
    tall = rows + 16
    f32 = jnp.float32
    anywhere = pl.BlockSpec(memory_space=pl.ANY)
    in_vmem = pl.BlockSpec(memory_space=pltpu.VMEM)
    back, rank = pl.pallas_call(
        functools.partial(facet_kernel, threshold),
        out_shape=(
            jax.ShapeDtypeStruct(image_cube.shape, f32),
            jax.ShapeDtypeStruct((channels, pixels), f32),
        ),
        in_specs=[anywhere, in_vmem],
        out_specs=(in_vmem, in_vmem),
        scratch_shapes=[
            pltpu.VMEM((channels, tall, cols), f32),
            pltpu.VMEM((3, channels, rows, cols), f32),
            pltpu.VMEM((3, rows, cols), f32),
            pltpu.VMEM((3, rows, cols), f32),
            pltpu.VMEM((2, channels, tall, cols), f32),
            pltpu.VMEM((order, pixels), f32),
            pltpu.VMEM((order, 128), f32),
            pltpu.VMEM((order, 128), f32),
            pltpu.VMEM((order, 128), f32),
            pltpu.VMEM((2, tall, 128), f32),
            pltpu.VMEM((2, tall, 128), f32),
            pltpu.VMEM((2, 2, tall, 128), f32),
            pltpu.VMEM((2, 2, tall, 128), f32),
            pltpu.SemaphoreType.DMA((12,)),
            pltpu.SemaphoreType.DMA((12,)),
            pltpu.SemaphoreType.DMA((1,)),
        ],
        compiler_params=pltpu.CompilerParams(
            collective_id=0, has_side_effects=True, vmem_limit_bytes=50 * 2**20
        ),
    )(image_cube, weights)
    return back, rank.reshape(image_cube.shape)


def solution(mesh):
    placed = (P("chan", "frow", "fcol"), P(None, "frow", "fcol"))
    return jax.shard_map(
        shards,
        mesh=mesh,
        in_specs=placed,
        out_specs=(P("chan", "frow", "fcol"), P("chan", "frow", "fcol")),
        check_vma=False,
    )
```

```python
import functools
import math

import jax
import jax.numpy as jnp
from jax import lax
from jax.experimental import pallas as pl
from jax.experimental.pallas import tpu as pltpu
from jax.sharding import PartitionSpec as P

JSWEEPS = 3


filter_taps = (0.0625, 0.25, 0.375, 0.25, 0.0625)
band_levels = (12.0, 4.0, 2.5)
rank_level = 2.0
tiny_value = 1e-30


def rank_round(state, marks):
    quads, sides, labels, cosine, sine = state
    eye, lane, row, first_mask, last_mask, step_mask, last = marks
    upper_left, upper_right, lower_left, lower_right = quads
    side_top, side_bottom = sides
    label_top, label_bottom = labels

    def across(values):
        return jnp.sum(jnp.where(eye, values, 0.0), axis=0, keepdims=True)

    cosine_row = across(cosine)
    sine_row = across(sine)

    def turn_rows(top, bottom):
        return cosine * top - sine * bottom, sine * top + cosine * bottom

    def move_rows(top, bottom):
        up = pltpu.roll(jnp.where(row == 0, bottom, top), 1, 0)
        down = pltpu.roll(bottom, last, 0)
        return jnp.where(row == 0, top, up), jnp.where(row == last, top, down)

    def turn_cols(left, right):
        return cosine_row * left - sine_row * right, sine_row * left + cosine_row * right

    def move_cols(left, right):
        ahead = pltpu.roll(jnp.where(lane == 0, right, left), 1, 1)
        back = pltpu.roll(right, lane.shape[1] - 1, 1)
        return jnp.where(lane == 0, left, ahead), jnp.where(lane == last, left, back)

    upper_left, lower_left = move_rows(*turn_rows(upper_left, lower_left))
    upper_right, lower_right = move_rows(*turn_rows(upper_right, lower_right))
    upper_left, upper_right = turn_cols(upper_left, upper_right)
    lower_left, lower_right = turn_cols(lower_left, lower_right)
    sides = move_rows(*turn_rows(side_top, side_bottom))
    label_top, label_bottom = move_rows(label_top, label_bottom)
    own_top = jnp.where(step_mask, upper_left, jnp.where(first_mask, upper_right, 0.0))
    next_mask = lane == row + 1
    own_bottom = jnp.where(
        next_mask & (row < last), lower_right, jnp.where(last_mask, lower_left, 0.0)
    )
    pair = jnp.where(next_mask & (row < last), upper_right, jnp.where(last_mask, upper_left, 0.0))
    gap = jnp.sum(own_bottom - own_top, axis=1, keepdims=True)
    cross = jnp.sum(pair, axis=1, keepdims=True)
    cosine, sine = turn_of(gap, cross, label_top < label_bottom)
    upper = move_cols(upper_left, upper_right)
    lower = move_cols(lower_left, lower_right)
    return (upper + lower, sides, (label_top, label_bottom), cosine, sine)


def turn_of(gap, cross, ordered):
    gap = jnp.broadcast_to(gap, ordered.shape)
    cross = jnp.broadcast_to(cross, ordered.shape)
    positive = (gap > 0) | ((gap == 0) & ordered)
    double = 2.0 * cross
    root = jnp.sqrt(gap * gap + double * double)
    tangent = jnp.where(positive, double, -double) / (jnp.abs(gap) + root + tiny_value)
    cosine = lax.rsqrt(1.0 + tangent * tangent)
    return cosine, tangent * cosine


def rank_start(gram):
    order = gram.shape[0]
    half, last, lanes = order // 2, order // 2 - 1, 128
    highest = lax.Precision.HIGHEST
    row = lax.broadcasted_iota(jnp.int32, (half, lanes), 0)
    lane = lax.broadcasted_iota(jnp.int32, (half, lanes), 1)
    eye = lane == row
    first_mask = (row == 1) & (lane == 0)
    last_mask = (row == last) & (lane == last)
    step_mask = ((row == 0) & (lane == 0)) | ((row >= 2) & (lane == row - 1))
    marks = (eye, lane, row, first_mask, last_mask, step_mask, last)
    mirror = lane == order - 1 - row
    pick_row = lax.broadcasted_iota(jnp.int32, (order, lanes), 0)
    pick_lane = lax.broadcasted_iota(jnp.int32, (order, lanes), 1)
    one = lambda mask: jnp.where(mask, 1.0, 0.0)
    pick_left = one((pick_row == pick_lane) & (pick_lane < half))
    pick_right = one((pick_row == order - 1 - pick_lane) & (pick_lane < half))
    dot = functools.partial(jnp.dot, precision=highest, preferred_element_type=jnp.float32)
    flip_row = lax.broadcasted_iota(jnp.int32, (half, half), 0)
    flip_lane = lax.broadcasted_iota(jnp.int32, (half, half), 1)
    flip = one(flip_row + flip_lane == last)
    top, bottom = gram[:half], dot(flip, gram[half:])
    quads = (dot(top, pick_left), dot(top, pick_right), dot(bottom, pick_left), dot(bottom, pick_right))
    sides = (one(eye), one(mirror))
    labels = (row, order - 1 - row)
    total = lambda values: jnp.sum(jnp.where(eye, values, 0.0), axis=1, keepdims=True)
    cosine, sine = turn_of(
        total(quads[3] - quads[0]), total(quads[1]), labels[0] < labels[1]
    )
    return (quads, sides, labels, cosine, sine), marks


def rank_finish(state, marks, threshold):
    highest = lax.Precision.HIGHEST
    eye = marks[0]
    total = lambda values: jnp.sum(jnp.where(eye, values, 0.0), axis=1, keepdims=True)
    quads, sides = state[0], state[1]
    mixing = 0.0
    for quad, side in zip((quads[0], quads[3]), sides):
        values = total(quad)
        factor = 1.0 - threshold / jnp.sqrt(jnp.maximum(values, threshold * threshold))
        mixing = mixing + lax.dot_general(
            side * factor, side, (((0,), (0,)), ((), ())), precision=highest,
            preferred_element_type=jnp.float32,
        )
    order = 2 * eye.shape[0]
    return mixing[:order, :order]


def spread(x, dilation):
    for axis in (0, 1):
        size = x.shape[axis]
        pair = x + pltpu.roll(x, 2 * dilation, axis)
        ends = pair + pltpu.roll(pair, size - 2 * dilation, axis)
        x = ends + 4.0 * (x + pltpu.roll(pair, size - dilation, axis))
    return x * (filter_taps[0] * filter_taps[0])


def split_two(values):
    high = values.astype(jnp.bfloat16)
    low = (values - high.astype(jnp.float32)).astype(jnp.bfloat16)
    return high, low


def facet_kernel(
    threshold, image_ref, weights_ref, back_ref, rank_ref,
    weight_scratch, wide, bands, sums, other_sums, diffs, full, gram, other_gram, mixing,
    pack_out, pack_in, pack_out_two, pack_in_two, send_sems, recv_sems, local_sems,
):
    channels, rows, cols = image_ref.shape
    pixels = rows * cols
    part = pixels // 2
    names = ("frow", "fcol", "chan")
    place = {name: lax.axis_index(name) for name in names}
    count = {name: lax.axis_size(name) for name in names}
    me = place["chan"]
    partner = 1 - me
    has = {
        ("frow", 1): place["frow"] < count["frow"] - 1,
        ("frow", -1): place["frow"] > 0,
        ("fcol", 1): place["fcol"] < count["fcol"] - 1,
        ("fcol", -1): place["fcol"] > 0,
    }
    barrier = pltpu.get_barrier_semaphore()
    mesh_ids = pl.DeviceIdType.MESH

    def target(name, step):
        ids = dict(place)
        ids[name] = place[name] + step
        return tuple(ids[key] for key in names)

    def mate():
        return (place["frow"], place["fcol"], partner)

    def copy_to(index, source, sink, device):
        return pltpu.make_async_remote_copy(
            src_ref=source, dst_ref=sink, send_sem=send_sems.at[index],
            recv_sem=recv_sems.at[index], device_id=device, device_id_type=mesh_ids,
        )

    own_rows = pl.ds(pl.multiple_of(me * channels, channels), channels)
    to_mate = pl.ds(pl.multiple_of(partner * part, part), part)
    keep_image = pltpu.make_async_copy(
        image_ref, wide.at[:, pl.ds(8, rows), :], local_sems.at[0]
    )
    keep_weights = pltpu.make_async_copy(weights_ref, weight_scratch, local_sems.at[1])
    keep_image.start()
    keep_weights.start()

    zero_rows = jnp.zeros((channels, 8, cols), jnp.float32)

    @pl.when(jnp.logical_not(has["frow", -1]))
    def _():
        wide[:, 0:8, :] = zero_rows
        diffs[0, :, 0:8, :] = zero_rows
        diffs[1, :, 0:8, :] = zero_rows

    @pl.when(jnp.logical_not(has["frow", 1]))
    def _():
        wide[:, rows + 8 : rows + 16, :] = zero_rows
        diffs[0, :, rows + 8 : rows + 16, :] = zero_rows
        diffs[1, :, rows + 8 : rows + 16, :] = zero_rows

    for side, step in ((0, -1), (1, 1)):

        @pl.when(jnp.logical_not(has["fcol", step]))
        def _(side=side):
            pack_in[side] = jnp.zeros(pack_in.shape[1:], jnp.float32)
            pack_in_two[side] = jnp.zeros(pack_in_two.shape[1:], jnp.float32)

    pl.semaphore_signal(barrier, inc=1, device_id=mate(), device_id_type=mesh_ids)
    friends = 1
    for key in has:

        @pl.when(has[key])
        def _(key=key):
            pl.semaphore_signal(barrier, inc=1, device_id=target(*key), device_id_type=mesh_ids)

        friends = friends + jnp.where(has[key], 1, 0)

    first_part = copy_to(0, full.at[own_rows, to_mate], full.at[own_rows, to_mate], mate())
    piece = part // 8
    early = pl.ds(pl.multiple_of(me * part, piece), piece)
    later = pl.ds(pl.multiple_of(me * part + piece, piece), part - piece)
    early_part = copy_to(12, full.at[own_rows, early], full.at[own_rows, early], mate())
    second_part = copy_to(1, full.at[own_rows, later], full.at[own_rows, later], mate())
    below = lambda ref, at: ref.at[..., pl.ds(at, 8), :]

    def row_copies(index, source, offset, sink):
        return (
            (("frow", 1), ("frow", -1), copy_to(
                index, below(source, offset + rows - 8), below(sink, 0), target("frow", 1))),
            (("frow", -1), ("frow", 1), copy_to(
                index + 1, below(source, offset), below(sink, rows + 8), target("frow", -1))),
        )

    def col_copies(index, source, sink):
        return (
            (("fcol", 1), ("fcol", -1), copy_to(
                index, source.at[1], sink.at[0], target("fcol", 1))),
            (("fcol", -1), ("fcol", 1), copy_to(
                index + 1, source.at[0], sink.at[1], target("fcol", -1))),
        )

    def start_all(copies):
        for goes, _, copy in copies:

            @pl.when(has[goes])
            def _(copy=copy):
                copy.start()

    def arrive_all(copies):
        for _, comes, copy in copies:

            @pl.when(has[comes])
            def _(copy=copy):
                copy.wait_recv()

    def left_all(copies):
        for goes, _, copy in copies:

            @pl.when(has[goes])
            def _(copy=copy):
                copy.wait_send()

    rows_one = row_copies(2, image_ref, 0, wide)
    cols_one = col_copies(4, pack_out, pack_in)
    rows_two = row_copies(8, diffs, 8, diffs)
    cols_two = col_copies(10, pack_out_two, pack_in_two)
    keep_image.wait()

    def flatten(at):
        group = jnp.swapaxes(wide[:, pl.ds(pl.multiple_of(at + 8, 8), 8), :], 0, 1)
        for row in range(8):
            where = pl.multiple_of((at + row) * cols, cols)
            full[own_rows, pl.ds(where, cols)] = group[row]

    def flatten_part(which):
        def body(step, carried):
            flatten(pl.multiple_of(which * (rows // 2) + step * 8, 8))
            return carried

        lax.fori_loop(0, rows // 16, body, 0)

    flatten_part(partner)
    pl.semaphore_wait(barrier, friends)
    first_part.start()
    start_all(rows_one)
    flatten_part(me)
    early_part.start()

    tall = rows + 16
    tile_lane = lax.broadcasted_iota(jnp.int32, (tall, 128), 1)

    def pack_edges(load, store):
        def body(ch, sides):
            left, right = sides
            here = (tile_lane >= ch * 8) & (tile_lane < ch * 8 + 8)
            tile_first = pltpu.roll(load(ch, pl.ds(0, 128)), ch * 8, 1)
            tile_last = pltpu.roll(load(ch, pl.ds(cols - 128, 128)), ch * 8 + 8, 1)
            return jnp.where(here, tile_first, left), jnp.where(here, tile_last, right)

        empty = jnp.zeros((tall, 128), jnp.float32)
        left, right = lax.fori_loop(0, channels, body, (empty, empty))
        store(0, left)
        store(1, right)

    def edge_tile(ch, before, after):
        after = pltpu.roll(after, 128 - ch * 8, 1)
        before = pltpu.roll(before, 120 - ch * 8, 1)
        return jnp.where(tile_lane < 8, after, jnp.where(tile_lane >= 120, before, 0.0))

    long = cols + 128
    row_at = lax.broadcasted_iota(jnp.int32, (tall, long), 0) - 8
    col_at = lax.broadcasted_iota(jnp.int32, (tall, long), 1)
    col_at = jnp.where(col_at < cols + 64, col_at, col_at - long)
    row_at = row_at + place["frow"] * rows
    col_at = col_at + place["fcol"] * cols
    valid = (row_at >= 0) & (row_at < count["frow"] * rows)
    valid = valid & (col_at >= 0) & (col_at < count["fcol"] * cols)
    inside = lambda values: jnp.where(valid, values, 0.0)

    arrive_all(rows_one)
    pack_edges(lambda ch, at: wide[ch, :, at], pack_out.__setitem__)
    start_all(cols_one)
    sums[...] = jnp.zeros(sums.shape, jnp.float32)
    arrive_all(cols_one)

    def analyse(ch, carried):
        center = wide[ch]
        tile = edge_tile(ch, pack_in[0], pack_in[1])
        coarse_one = inside(spread(jnp.concatenate([center, tile], axis=1), 1))
        coarse_two = spread(coarse_one, 2)[8 : rows + 8, :cols]
        coarse_one = coarse_one[8 : rows + 8, :cols]
        for index, band in enumerate(
            (center[8 : rows + 8] - coarse_one, coarse_one - coarse_two, coarse_two)
        ):
            bands[index, ch] = band
            sums[index] = sums[index] + band * band
        return carried

    lax.fori_loop(0, channels, analyse, 0)
    share_sums = copy_to(6, sums, other_sums, mate())

    first_part.wait_recv()
    order = 2 * channels
    block = 1024
    start = me * part

    def gram_step(step, total):
        at = pl.ds(pl.multiple_of(start + step * block, block), block)
        both = jnp.concatenate(split_two(full[:, at]), axis=0)
        return total + lax.dot_general(
            both, both, (((1,), (1,)), ((), ())), preferred_element_type=jnp.float32
        )

    product = lax.fori_loop(
        0, part // block, gram_step, jnp.zeros((2 * order, 2 * order), jnp.float32)
    )
    gram[:, :order] = (
        product[:order, :order] + (product[:order, order:] + product[order:, :order])
    ) + product[order:, order:]
    share_gram = copy_to(7, gram, other_gram, mate())
    share_gram.start()

    share_sums.start()
    second_part.start()

    share_gram.wait_recv()
    state, marks = rank_start(gram[:, :order] + other_gram[:, :order])
    rounds = JSWEEPS * (order - 1)
    turn = lambda _, carried: rank_round(carried, marks)
    state = lax.fori_loop(0, 3 * rounds // 10, turn, state)
    share_sums.wait_recv()
    keep_weights.wait()
    for index in range(3):
        levels = band_levels[index] * weight_scratch[index]
        totals = sums[index] + other_sums[index]
        other_sums[index] = levels / jnp.sqrt(jnp.maximum(totals, levels * levels))

    def project(ch, carried):
        duals = [bands[index, ch] * other_sums[index] for index in range(3)]
        back_ref[ch] = duals[0]
        diffs[0, ch, pl.ds(8, rows), :] = duals[1] - duals[0]
        diffs[1, ch, pl.ds(8, rows), :] = duals[2] - duals[1]
        return carried

    lax.fori_loop(0, channels, project, 0)
    start_all(rows_two)
    state = lax.fori_loop(3 * rounds // 10, 8 * rounds // 10, turn, state)
    arrive_all(rows_two)
    for index in range(2):
        pack_edges(
            lambda ch, at, index=index: diffs[index, ch, :, at],
            lambda side, value, index=index: pack_out_two.__setitem__((side, index), value),
        )
    start_all(cols_two)
    state = lax.fori_loop(8 * rounds // 10, rounds, turn, state)
    mixing[:, :order] = rank_finish(state, marks, threshold)

    high, low = split_two(mixing[own_rows, :order])
    left = jnp.concatenate([high, high, low, low], axis=1)

    def rank_part(which):
        def body(step, carried):
            at = pl.ds(pl.multiple_of(which * part + step * block, block), block)
            high, low = split_two(full[:, at])
            right = jnp.concatenate([high, low, high, low], axis=0)
            rank_ref[:, at] = jnp.dot(left, right, preferred_element_type=jnp.float32)
            return carried

        lax.fori_loop(0, part // block, body, 0)

    rank_part(me)
    arrive_all(cols_two)

    def synthesise(ch, carried):
        outer, inner = [
            jnp.concatenate(
                [diffs[index, ch], edge_tile(ch, pack_in_two[0, index], pack_in_two[1, index])],
                axis=1,
            )
            for index in range(2)
        ]
        summed = inside(outer + spread(inner, 2))
        back_ref[ch] = back_ref[ch] + spread(summed, 1)[8 : rows + 8, :cols]
        return carried

    lax.fori_loop(0, channels, synthesise, 0)

    early_part.wait_recv()
    second_part.wait_recv()
    rank_part(partner)
    for copies in (rows_one, cols_one, rows_two, cols_two):
        left_all(copies)
    for copy in (first_part, early_part, second_part, share_sums, share_gram):
        copy.wait_send()


def shards(image_cube, weights):
    channels, rows, cols = image_cube.shape
    pixels = rows * cols
    threshold = rank_level * math.sqrt(pixels)
    order = channels * lax.axis_size("chan")
    tall = rows + 16
    f32 = jnp.float32
    far = pl.BlockSpec(memory_space=pltpu.HBM)
    in_vmem = pl.BlockSpec(memory_space=pltpu.VMEM)
    back, rank = pl.pallas_call(
        functools.partial(facet_kernel, threshold),
        out_shape=(
            jax.ShapeDtypeStruct(image_cube.shape, f32),
            jax.ShapeDtypeStruct((channels, pixels), f32),
        ),
        in_specs=[far, far],
        out_specs=(in_vmem, in_vmem),
        scratch_shapes=[
            pltpu.VMEM((3, rows, cols), f32),
            pltpu.VMEM((channels, tall, cols), f32),
            pltpu.VMEM((3, channels, rows, cols), f32),
            pltpu.VMEM((3, rows, cols), f32),
            pltpu.VMEM((3, rows, cols), f32),
            pltpu.VMEM((2, channels, tall, cols), f32),
            pltpu.VMEM((order, pixels), f32),
            pltpu.VMEM((order, 128), f32),
            pltpu.VMEM((order, 128), f32),
            pltpu.VMEM((order, 128), f32),
            pltpu.VMEM((2, tall, 128), f32),
            pltpu.VMEM((2, tall, 128), f32),
            pltpu.VMEM((2, 2, tall, 128), f32),
            pltpu.VMEM((2, 2, tall, 128), f32),
            pltpu.SemaphoreType.DMA((13,)),
            pltpu.SemaphoreType.DMA((13,)),
            pltpu.SemaphoreType.DMA((2,)),
        ],
        compiler_params=pltpu.CompilerParams(
            collective_id=0, has_side_effects=True, vmem_limit_bytes=50 * 2**20
        ),
    )(image_cube, weights)
    return back, rank.reshape(image_cube.shape)


def solution(mesh):
    placed = (P("chan", "frow", "fcol"), P(None, "frow", "fcol"))
    return jax.shard_map(
        shards,
        mesh=mesh,
        in_specs=placed,
        out_specs=(P("chan", "frow", "fcol"), P("chan", "frow", "fcol")),
        check_vma=False,
    )
```
